32 devices in a mesh: slab: 4 (over y, x), row: 8 (over z, core).
Axes of the slice: x: 2, y: 2, z: 4, core: 2. Of those that a mesh axis runs over, the one named last changes fastest.
Arguments:
- psi: float32 [20, 2304, 2048], P('slab', 'row'), may hold values from -6 to 6
- ritz: float32 [2048, 512], P(('slab', 'row')), may hold values from -0.125 to 0.125
- ritz_values: float32 [512], P('row'), may hold values from -2 to 4
- potential: float32 [20, 2304], P('slab'), may hold values from -1.5 to 1.5
Outputs:
- residual: float32 [512, 20, 2304], P('row', 'slab')
The draws below stay inside these ranges and needn't reach their ends.
All inputs are finite; a program needn't handle non-finite values.
Results may differ from the reference program's by a relative error of at most 0.00007.
Values sent between devices are 32-bit elements; how exact they have to be, the bound alone decides.
No kernel may reach another device: no remote copies, remote signals or barrier semaphores. Data moves between devices by JAX's collectives and lax.ppermute only.
A program may use at most 64 MiB of HBM per device.

```python
import jax
import jax.numpy as jnp
from jax import lax

NS = 2048
M = 512
NX = 48
NY = 48
NZ = 20
NXY = 2304


def levels(rng, dims, cuts, least, high):
    def one(position, parts):
        heights = jax.random.uniform(jax.random.fold_in(jax.random.fold_in(rng, 6), position), (parts,), jnp.float32, least / len(cuts), high / len(cuts))
        return jnp.repeat(jnp.exp(heights), dims[position] // parts).reshape((-1,) + (1,) * (len(dims) - position - 1))

    level = one(*cuts[0])
    for cut in cuts[1:]:
        level = level * one(*cut)
    return level


def bell_draw(stream_key, shape, deviation, reach, cuts=(), held_as=jnp.bfloat16):
    entries = deviation * jax.random.normal(stream_key, shape, jnp.float32)
    if cuts:
        entries = entries * levels(stream_key, shape, cuts, -0.22, 0.18)
    return jnp.clip(entries, -reach, reach).astype(held_as)


def setup_inputs(seed: int = 0) -> dict:
    splits = jax.random.split(jax.random.key(seed), 5)
    return {
        "psi": bell_draw(splits[0], (NZ, NXY, NS), 1.0, 6.0, ((0, 4), (1, 8)), jnp.float32),
        "ritz": bell_draw(splits[1], (NS, M), NS ** -0.5, 0.125, ((0, 32),), jnp.float32),
        "ritz_values": jnp.clip(-2.0 + 6.0 * jax.random.uniform(splits[2], (M,), jnp.float32) ** levels(splits[2], (M,), ((0, 8),), -0.2, 0.2), -2.0, 4.0),
        "potential": jnp.clip(jax.random.uniform(splits[3], (NZ, NXY), jnp.float32, -1.5, 1.5) * levels(splits[3], (NZ, NXY), ((0, 4),), -0.4, 0.0), -1.5, 1.5),
    }


coefs = (-1.0 / 12.0, 4.0 / 3.0, -2.5, 4.0 / 3.0, -1.0 / 12.0)


def along(padded, axis, count):
    total = coefs[0] * lax.slice_in_dim(padded, 0, count, axis=axis)
    for shift in range(1, 5):
        total = total + coefs[shift] * lax.slice_in_dim(padded, shift, shift + count, axis=axis)
    return total


def laplace(field):
    total = along(jnp.pad(field, ((2, 2), (0, 0), (0, 0))), 0, field.shape[0])
    total = total + along(jnp.pad(field, ((0, 0), (2, 2), (0, 0))), 1, field.shape[1])
    total = total + along(jnp.pad(field, ((0, 0), (0, 0), (2, 2))), 2, field.shape[2])
    return total


def reference(psi, ritz, ritz_values, potential):
    def rotate_plane(plane):
        return jnp.dot(plane, ritz, precision=lax.Precision.HIGHEST, preferred_element_type=jnp.float32)

    rotated = lax.map(rotate_plane, psi)
    rotated = jnp.transpose(rotated, (2, 0, 1))
    pot_grid = potential.reshape(NZ, NY, NX)

    def one_state(pair):
        state, value = pair
        field = state.reshape(NZ, NY, NX)
        result = -0.5 * laplace(field) + pot_grid * field - value * field
        return result.reshape(NZ, NXY)

    return lax.map(one_state, (rotated, ritz_values))
```

```python
import functools

import jax
import jax.numpy as jnp
from jax import lax
from jax.experimental import pallas as pl
from jax.experimental.pallas import tpu as pltpu
from jax.sharding import PartitionSpec as P

NX = 48
NY = 48
LANES = 128
HALF = 64

coefs = (-1.0 / 12.0, 4.0 / 3.0, -2.5, 4.0 / 3.0, -1.0 / 12.0)


VMEM = pl.BlockSpec(memory_space=pltpu.VMEM)
SMEM = pl.BlockSpec(memory_space=pltpu.SMEM)
ANY = pl.BlockSpec(memory_space=pl.ANY)


def padded_2(block, sides, width):
    for axis, dim in sides:
        count = lax.axis_size(axis)
        forward = [(i, i + 1) for i in range(count - 1)]
        backward = [(target, source) for source, target in forward]
        low = lax.ppermute(
            lax.slice_in_dim(block, block.shape[dim] - width, None, axis=dim), axis, forward
        )
        high = lax.ppermute(lax.slice_in_dim(block, 0, width, axis=dim), axis, backward)
        block = jnp.concatenate([low, block, high], axis=dim)
    return block


def along(padded, axis, count):
    total = coefs[0] * lax.slice_in_dim(padded, 0, count, axis=axis)
    for shift in range(1, 5):
        total = total + coefs[shift] * lax.slice_in_dim(padded, shift, shift + count, axis=axis)
    return total


def residual_of(extended, potential, values):
    states, planes_ext, points = extended.shape
    planes = planes_ext - 4
    grid = extended.reshape(states, planes_ext, NY, NX)
    center = grid[:, 2 : 2 + planes]
    lap = along(grid, 1, planes)
    lap = lap + along(jnp.pad(center, ((0, 0), (0, 0), (2, 2), (0, 0))), 2, NY)
    lap = lap + along(jnp.pad(center, ((0, 0), (0, 0), (0, 0), (2, 2))), 3, NX)
    pot_grid = potential.reshape(planes, NY, NX)
    result = -0.5 * lap + pot_grid[None] * center - values[:, None, None, None] * center
    return result.reshape(states, planes, points)


def plain(psi, ritz, ritz_values, potential):
    whole_ritz = lax.all_gather(ritz, ("slab", "row"), axis=0, tiled=True)
    rotated = lax.dot_general(
        whole_ritz,
        psi,
        (((0,), (2,)), ((), ())),
        precision=lax.Precision.HIGHEST,
        preferred_element_type=jnp.float32,
    )
    owned = lax.all_to_all(rotated, "row", split_axis=0, concat_axis=2, tiled=True)
    extended = padded_2(owned, (("slab", 1),), 2)
    return residual_of(extended, potential, ritz_values)


def swap(array, axis, offset):
    count = lax.axis_size(axis)
    return lax.ppermute(array, axis, [(i, i ^ offset) for i in range(count)])


def shifted(array, axis, step):
    count = lax.axis_size(axis)
    pairs = [(i, i + step) for i in range(count) if 0 <= i + step < count]
    return lax.ppermute(array, axis, pairs)


def blocks_by_distance(ids, ritz, chips, groups):
    rows = ritz.shape[0]

    def kernel(ids_ref, ritz_ref, *outs):
        place = 0
        for group in groups:
            for far in range(chips):
                for slot, offset in enumerate(group):
                    block = jnp.bitwise_xor(ids_ref[1], far ^ offset)
                    start = pl.multiple_of(block * LANES, LANES)
                    outs[place][slot] = ritz_ref[:, pl.ds(start, LANES)]
                place += 1

    shapes = [
        jax.ShapeDtypeStruct((len(group), rows, LANES), jnp.float32)
        for group in groups
        for _ in range(chips)
    ]
    flat = pl.pallas_call(
        kernel, out_shape=shapes, in_specs=[SMEM, VMEM], out_specs=[VMEM] * len(shapes), name="blocks"
    )(ids, ritz)
    return [flat[g * chips : (g + 1) * chips] for g in range(len(groups))]


def gather_rows(parts, slabs):
    column = jnp.stack([parts[0]] + [swap(parts[far], "row", 2 * far) for far in range(1, len(parts))])
    plane = jnp.stack([column] + [swap(column, "slab", far) for far in range(1, slabs)])
    return plane, swap(plane, "row", 1)


def rotate(ids, mine, other, psi, splits):
    slabs, chips, count, rows, _ = mine.shape
    planes, points, depth = psi.shape
    half = points // 2
    width = count * LANES

    def kernel(ids_ref, mine_ref, other_ref, psi_ref, *rest):
        outs, (weights, total) = rest[:-2], rest[-2:]
        step = pl.program_id(0)
        core = ids_ref[2]

        @pl.when(step == 0)
        def _():
            for side, ref in ((0, mine_ref), (1, other_ref)):
                for s in range(slabs):
                    for z in range(chips):
                        owner = jnp.bitwise_xor(ids_ref[0], s) * chips + jnp.bitwise_xor(ids_ref[1], z)
                        owner = owner * 2 + jnp.bitwise_xor(core, side)
                        at = pl.ds(pl.multiple_of(owner * rows, rows), rows)
                        for slot in range(count):
                            block = ref[s, z, slot]
                            block = jnp.where(core == 1, pltpu.roll(block, HALF, 1), block)
                            high = block.astype(jnp.bfloat16)
                            low = (block - high.astype(jnp.float32)).astype(jnp.bfloat16)
                            weights[at, slot * LANES : (slot + 1) * LANES] = high
                            weights[at, width + slot * LANES : width + (slot + 1) * LANES] = low

        block = psi_ref[0]
        high = block.astype(jnp.bfloat16)
        low = (block - high.astype(jnp.float32)).astype(jnp.bfloat16)
        wide = jnp.dot(high, weights[...], preferred_element_type=jnp.float32)
        rest_ = jnp.dot(low, weights[:, :width], preferred_element_type=jnp.float32)
        total[step] = wide[:, :width] + (wide[:, width:] + rest_)

        @pl.when(step == planes - 1)
        def _():
            place = 0

            def pair(first, second, side):
                lane = lax.broadcasted_iota(jnp.int32, first.shape, 1) < HALF
                if side == 0:
                    return jnp.where(lane, first, pltpu.roll(second, HALF, 1))
                return jnp.where(lane, pltpu.roll(first, HALF, 1), second)

            for slot, split in enumerate(splits):
                lanes = slice(slot * LANES, (slot + 1) * LANES)
                for side in range(2):
                    out = outs[place]
                    out[0:points] = pair(total[0, :, lanes], total[1, :, lanes], side)
                    out[points : 2 * points] = pair(total[3, :, lanes], total[4, :, lanes], side)
                    middle = pair(total[2, :half, lanes], total[2, half:, lanes], side)
                    if split:
                        outs[place + 1][...] = middle
                        place += 2
                    else:
                        out[2 * points :] = middle
                        place += 1

    shapes = []
    for split in splits:
        for _ in range(2):
            sizes = (2 * points, half) if split else (2 * points + half,)
            shapes += [jax.ShapeDtypeStruct((size, LANES), jnp.float32) for size in sizes]
    whole = pl.BlockSpec(mine.shape, lambda i: (0,) * 5, pipeline_mode=pl.Buffered(1))
    flat = pl.pallas_call(
        kernel,
        grid=(planes,),
        out_shape=shapes,
        in_specs=[SMEM, whole, whole, pl.BlockSpec((1, points, depth), lambda i: (i, 0, 0))],
        out_specs=[pl.BlockSpec(shape.shape, lambda i: (0, 0)) for shape in shapes],
        scratch_shapes=[
            pltpu.VMEM((depth, 2 * width), jnp.bfloat16),
            pltpu.VMEM((planes, points, width), jnp.float32),
        ],
        compiler_params=pltpu.CompilerParams(vmem_limit_bytes=40 << 20),
        cost_estimate=pl.CostEstimate(
            flops=6 * planes * points * depth * width,
            bytes_accessed=4 * planes * points * depth,
            transcendentals=0,
        ),
        name="rotate",
    )(ids, mine, other, psi)
    flat = list(flat)
    pieces = []
    for split in splits:
        sides = []
        for _ in range(2):
            if split:
                sides.append((flat.pop(0), flat.pop(0)))
            else:
                sides.append((flat.pop(0),))
        pieces.append(sides)
    return pieces


def stencil(ids, pieces, halos, potential, values, shape):
    states, planes, grid_points = shape
    chips = len(pieces)
    sources = 2 * chips
    points = grid_points // sources
    half = points // 2
    pad = 2 * NX
    rows_at_once = 8
    span = rows_at_once * NX
    steps = NY // rows_at_once
    flat = []
    where = {}
    for k in range(chips):
        for side in range(2):
            arrays = pieces[k][side]
            where[k, side] = [(len(flat) + i) for i in range(len(arrays))]
            flat += list(arrays)
    first_halo = len(flat)
    for low, high in halos:
        flat += [low, high]
    arrays = len(flat)

    def kernel(ids_ref, pot_ref, value_ref, *rest):
        refs, out = rest[:arrays], rest[arrays]
        below, pair_0, middle, pair_1, above, packed, made, sems = rest[arrays + 1 :]
        copies = []

        def copy(source, target):
            one = pltpu.make_async_copy(source, target, sems.at[len(copies)])
            one.start()
            copies.append(one)

        for k in range(chips):
            for side in range(2):
                owner = jnp.bitwise_xor(ids_ref[1] * 2 + ids_ref[2], 2 * k + side)
                start = pl.multiple_of(owner * points, 8)
                inner = pl.ds(pl.multiple_of(pad + owner * points, 8), points)
                at = where[k, side]
                main = refs[at[0]]
                copy(main.at[pl.ds(0, points)], pair_0.at[inner])
                copy(main.at[pl.ds(points, points)], pair_1.at[inner])
                if len(at) == 2:
                    copy(refs[at[1]], packed.at[owner])
                else:
                    copy(main.at[pl.ds(2 * points, half)], packed.at[owner])
                copy(refs[first_halo + 2 * k].at[side], below.at[pl.ds(start, points)])
                copy(refs[first_halo + 2 * k + 1].at[side], above.at[pl.ds(start, points)])
        zero = jnp.zeros((pad, LANES), jnp.float32)
        for field in (pair_0, middle, pair_1):
            field[0:pad] = zero
            field[pad + grid_points :] = zero
        for one in copies:
            one.wait()

        for owner in range(sources):
            block = packed[owner]
            turned = pltpu.roll(block, HALF, 1)
            lane = lax.broadcasted_iota(jnp.int32, block.shape, 1) < HALF
            base = pad + owner * points
            middle[base : base + half] = jnp.where(lane, block, turned)
            middle[base + half : base + points] = jnp.where(lane, turned, block)

        lane = lax.broadcasted_iota(jnp.int32, (NX, LANES), 1) < HALF
        x = lax.broadcasted_iota(jnp.int32, (NX, LANES), 0)
        value = jnp.broadcast_to(value_ref[...], (NX, LANES))

        def in_plane(field, base):
            f = field[pl.ds(base, NX), :]
            near = jnp.where(x >= 1, pltpu.roll(f, 1, 0), 0.0) + jnp.where(x < NX - 1, pltpu.roll(f, NX - 1, 0), 0.0)
            far = jnp.where(x >= 2, pltpu.roll(f, 2, 0), 0.0) + jnp.where(x < NX - 2, pltpu.roll(f, NX - 2, 0), 0.0)
            near += field[pl.ds(base - NX, NX), :] + field[pl.ds(base + NX, NX), :]
            far += field[pl.ds(base - 2 * NX, NX), :] + field[pl.ds(base + 2 * NX, NX), :]
            return f, near, far

        center, one_off, two_off = -0.5 * 3.0 * coefs[2], -0.5 * coefs[1], -0.5 * coefs[0]

        def body(step, _):
            def line(i, _):
                at = pl.multiple_of(step * span + i * NX, 8)
                base = pl.multiple_of(at + pad, 8)
                pot = pot_ref[pl.ds(at, NX), :]

                def spread(first, second):
                    first = jnp.broadcast_to(pot[:, first : first + 1], (NX, LANES))
                    second = jnp.broadcast_to(pot[:, second : second + 1], (NX, LANES))
                    return jnp.where(lane, first, second)

                def finish(slot, f, near, far, pot_):
                    made[slot, pl.ds(pl.multiple_of(i * NX, 8), NX), :] = (
                        (pot_ - value + center) * f + one_off * near + two_off * far
                    )

                a, e = below[pl.ds(at, NX), :], above[pl.ds(at, NX), :]
                b, b1, b2 = in_plane(pair_0, base)
                c, c1, c2 = in_plane(middle, base)
                d, d1, d2 = in_plane(pair_1, base)
                sa, sb = pltpu.roll(a, HALF, 1), pltpu.roll(b, HALF, 1)
                sd, se = pltpu.roll(d, HALF, 1), pltpu.roll(e, HALF, 1)
                finish(0, b, b1 + sb + jnp.where(lane, sa, c), b2 + a + jnp.where(lane, c, sd), spread(0, 1))
                finish(1, d, d1 + sd + jnp.where(lane, c, se), d2 + e + jnp.where(lane, sb, c), spread(3, 4))
                finish(2, c, c1 + sb + d, c2 + b + sd, spread(2, 2))
                return 0

            lax.fori_loop(0, rows_at_once, line, 0)
            for block in range(span // LANES):
                lanes = pl.ds(pl.multiple_of(step * span + block * LANES, LANES), LANES)
                for slot, targets in ((0, (0, 1)), (1, (3, 4)), (2, (2,))):
                    turned = jnp.transpose(made[slot, block * LANES : (block + 1) * LANES, :])
                    for side, plane in enumerate(targets):
                        out[:, plane, lanes] = turned[side * HALF : side * HALF + states]
            return 0

        lax.fori_loop(0, steps, body, 0)

    padded = grid_points + 2 * pad
    return pl.pallas_call(
        kernel,
        out_shape=jax.ShapeDtypeStruct(shape, jnp.float32),
        in_specs=[SMEM, VMEM, VMEM] + [ANY] * arrays,
        out_specs=VMEM,
        scratch_shapes=[
            pltpu.VMEM((grid_points, LANES), jnp.float32),
            pltpu.VMEM((padded, LANES), jnp.float32),
            pltpu.VMEM((padded, LANES), jnp.float32),
            pltpu.VMEM((padded, LANES), jnp.float32),
            pltpu.VMEM((grid_points, LANES), jnp.float32),
            pltpu.VMEM((sources, half, LANES), jnp.float32),
            pltpu.VMEM((3, span, LANES), jnp.float32),
            pltpu.SemaphoreType.DMA((5 * sources,)),
        ],
        compiler_params=pltpu.CompilerParams(vmem_limit_bytes=24 << 20),
        cost_estimate=pl.CostEstimate(
            flops=40 * states * planes * grid_points,
            bytes_accessed=16 * states * planes * grid_points,
            transcendentals=0,
        ),
        name="stencil",
    )(ids, potential, values, *flat)


def staged(psi, ritz, ritz_values, potential):
    slabs, chips = lax.axis_size("slab"), lax.axis_size("row") // 2
    planes, points, _ = psi.shape
    states = ritz.shape[1] // (2 * chips)
    grid_points = points * 2 * chips
    row = lax.axis_index("row")
    ids = jnp.stack([lax.axis_index("slab"), row // 2, row % 2]).astype(jnp.int32)
    pot = jnp.transpose(potential)
    values = jnp.concatenate([ritz_values, ritz_values])[None]

    groups = ((chips - 1,),) + (tuple(range(chips - 1)),)
    parts = blocks_by_distance(ids, ritz, chips, groups)
    pieces, halos = {}, {}
    for group, part in zip(groups, parts):
        mine, other = gather_rows(part, slabs)
        splits = [offset >= 2 for offset in group]
        made = rotate(ids, mine, other, psi, splits)
        for offset, sides in zip(group, made):
            pieces[offset] = [
                [swap(array, "row", 2 * offset + side) if offset or side else array for array in sides[side]]
                for side in range(2)
            ]
    for offset in range(chips):
        mains = [pieces[offset][side][0] for side in range(2)]
        up = jnp.stack([main[points : 2 * points] for main in mains])
        down = jnp.stack([main[:points] for main in mains])
        halos[offset] = (shifted(up, "slab", 1), shifted(down, "slab", -1))
    order = range(chips)
    return stencil(
        ids, [pieces[k] for k in order], [halos[k] for k in order], pot, values, (states, planes, grid_points)
    )


def power_of_two(count):
    return count & (count - 1) == 0


def local(psi, ritz, ritz_values, potential):
    slabs, rows = lax.axis_size("slab"), lax.axis_size("row")
    planes, points, depth = psi.shape
    fits = (
        power_of_two(slabs)
        and power_of_two(rows)
        and rows >= 4
        and planes == 5
        and 2 * ritz.shape[1] == rows * LANES
        and ritz.shape[0] % 16 == 0
        and points % 16 == 0
        and points * rows == NX * NY
        and points // 2 % 8 == 0
    )
    if fits:
        return staged(psi, ritz, ritz_values, potential)
    return plain(psi, ritz, ritz_values, potential)


def solution(mesh):
    in_specs = (P("slab", "row", None), P(("slab", "row"), None), P("row"), P("slab", None))
    out_specs = P("row", "slab", None)
    return jax.shard_map(local, mesh=mesh, in_specs=in_specs, out_specs=out_specs, check_vma=False)
```
